512 devices in a mesh: dom: 64 (over y, z), mode: 8 (over x, core).
Axes of the slice: x: 4, y: 4, z: 16, core: 2. Of those that a mesh axis runs over, the one named last changes fastest.
Arguments:
- mode_basis: bfloat16 [3, 512, 65536], P(None, 'mode', 'dom'), may hold values from -6 to 6
- blocks: bfloat16 [16, 3, 3, 65536], P(None, None, None, 'dom'), may hold values from -0.875 to 0.875
- columns: int32 [16, 65536], P(None, 'dom'), may hold values from -256 to 257, as said below
- samples: int32 [512], replicated, may hold values from 0 to 196607, as said below
- inverse: bfloat16 [512, 512], replicated, may hold values from -0.25 to 0.25
Outputs:
- reduced: float32 [512, 512], P('dom', 'mode')
- coefficients: float32 [512, 512], P('dom', 'mode')
The draws below stay inside these ranges and needn't reach their ends.
Inputs may be any that keep to these rules, and one draw needn't show every extreme that they name: `columns`: each entry is 256 + 1 (an empty slot) or an offset that keeps n + offset within 0 to 65535; slot 0 of every row holds offset 0. `samples`: 512 distinct dofs; half of them lie in the first half of the dofs.
All inputs are finite; a program needn't handle non-finite values.
Results may differ from the reference program's by a relative error of at most 0.0029.
Values may be sent and summed in bfloat16 or wider, within the bound.
No kernel may reach another device: no remote copies, remote signals or barrier semaphores. Data moves between devices by JAX's collectives and lax.ppermute only.
A program may use at most 64 MiB of HBM per device.

```python
import jax
import jax.numpy as jnp
from jax import lax

R = 512
SAMPLES = 512
NBR = 16
HB = 256
NN = 65536


def draw_columns(key, part):
    first_key, second_key = jax.random.split(jax.random.fold_in(key, 11))
    counts = jax.random.randint(first_key, (1, NN), NBR // 2, NBR + 1)
    offsets = jax.random.randint(second_key, (NBR, NN), -HB, HB + 1)
    slot_index = lax.broadcasted_iota(jnp.int32, (NBR, NN), 0)
    node_index = lax.broadcasted_iota(jnp.int32, (NBR, NN), 1)
    forced = (slot_index == 1) & (node_index == NN - 1)
    offsets = jnp.where(slot_index == 0, 0, offsets)
    offsets = jnp.where(forced, -HB, offsets)
    target = node_index + offsets
    usable = (slot_index < counts) & (target >= 0) & (target < NN)
    usable = usable | forced
    usable = usable & jnp.logical_not((slot_index == NBR - 1) & (node_index == 0))
    return jnp.where(usable, offsets, HB + 1).astype(jnp.int32)


def draw_samples(key, part):
    first_key, second_key = jax.random.split(jax.random.fold_in(key, 23))
    lower_count = 3 * NN // 2
    upper_count = 3 * NN - lower_count
    lower_half = SAMPLES // 2
    lower = jax.random.permutation(first_key, lower_count)[:lower_half]
    lower = (lower - lower[0]) % lower_count
    upper = jax.random.permutation(second_key, upper_count)[:SAMPLES - lower_half]
    upper = 3 * NN - 1 - (upper - upper[0]) % upper_count
    return jnp.concatenate([lower, upper]).astype(jnp.int32)


def block_scale(stream_key, dims, pieces, low, top_value):
    loudness, own = 1.0, jax.random.fold_in(stream_key, 6)
    for axis_at, shards_of in pieces:
        draws = jnp.exp(jax.random.uniform(jax.random.fold_in(own, axis_at), (shards_of,), jnp.float32, low / len(pieces), top_value / len(pieces)))
        loudness = loudness * jnp.repeat(draws, dims[axis_at] // shards_of).reshape([-1 if axis == axis_at else 1 for axis in range(len(dims))])
    return loudness


def bell_draw(key, extent, scale, bound, shards=(), kind=jnp.bfloat16):
    result = jax.random.normal(key, extent, jnp.float32) * scale
    if len(shards) > 0:
        result = block_scale(key, extent, shards, -0.22, 0.18) * result
    return jnp.clip(result, min=-bound, max=bound).astype(kind)


def setup_inputs(seed: int = 0) -> dict:
    streams_of = jax.random.split(jax.random.key(seed), 6)
    mode_basis = bell_draw(streams_of[0], (3, R, NN), 1.0, 6.0, ((1, 8), (2, 64)))
    blocks = bell_draw(streams_of[1], (NBR, 3, 3, NN), (3 * NBR) ** -0.5, 0.875, ((3, 64),))
    columns = draw_columns(jax.random.fold_in(streams_of[5], 71), 0)
    samples = draw_samples(jax.random.fold_in(streams_of[5], 71), 0)
    inverse = bell_draw(streams_of[4], (SAMPLES, SAMPLES), SAMPLES ** -0.5, 0.25)
    return dict(mode_basis=mode_basis, blocks=blocks, columns=columns, samples=samples, inverse=inverse)


def reference(mode_basis, blocks, columns, samples, inverse):
    node_ids = lax.broadcasted_iota(jnp.int32, (NN,), 0)

    def slot_step(slot_index, running):
        offset = columns[slot_index]
        usable = offset != HB + 1
        position = jnp.where(usable, node_ids + offset, 0).astype(jnp.int32)
        nearby = jnp.take(mode_basis, position, axis=2).astype(jnp.float32)
        weights = jnp.where(usable[None, None, :], blocks[slot_index].astype(jnp.float32), jnp.float32(0.0))
        running = running + weights[:, 0, None, :] * nearby[0][None]
        running = running + weights[:, 1, None, :] * nearby[1][None]
        running = running + weights[:, 2, None, :] * nearby[2][None]
        return running
    zero_image = jnp.zeros(mode_basis.shape, jnp.float32)
    image = lax.fori_loop(0, NBR, slot_step, zero_image).astype(jnp.bfloat16)
    reduced = jnp.tensordot(mode_basis.astype(jnp.float32), image.astype(jnp.float32), axes=((0, 2), (0, 2)), precision=lax.Precision.HIGHEST)
    reduced = reduced / jnp.sqrt(jnp.float32(3 * NN))
    component = samples % 3
    node_index = samples // 3
    picked = image[component, :, node_index]
    coefficients = jnp.dot(inverse, picked, preferred_element_type=jnp.float32)
    return (reduced, coefficients)
```

```python
import functools
import math

import jax
import jax.numpy as jnp
from jax import lax
from jax.experimental import pallas as pl
from jax.experimental.pallas import tpu as pltpu
from jax.sharding import Mesh, PartitionSpec as P

DOM = ("y", "z")
MODE = ("x", "core")
F32 = jnp.float32
BF16 = jnp.bfloat16
LANES = 128


def stencil_kernel(columns_ref, weights_ref, before_ref, basis_ref, after_ref, image_ref, extended_ref, target_ref):
    slots, nodes = columns_ref.shape
    parts, modes, halo = before_ref.shape
    window = LANES + 2 * halo
    chunks = window // LANES
    for b in range(parts):
        rows = slice(b * modes, (b + 1) * modes)
        extended_ref[rows, 0:halo] = before_ref[b]
        extended_ref[rows, halo : halo + nodes] = basis_ref[b]
        extended_ref[rows, halo + nodes :] = after_ref[b]
    lane = lax.broadcasted_iota(jnp.int32, (slots, LANES), 1)
    row_ids = lax.broadcasted_iota(jnp.int32, (16, LANES), 0)
    one = jnp.ones((16, LANES), BF16)
    zero = jnp.zeros((16, LANES), BF16)
    ids = [(row_ids + 16 * q).astype(F32).astype(BF16) for q in range(LANES // 16)]

    def node_block(step, carry):
        first = pl.multiple_of(step * LANES, LANES)
        here = pl.ds(first, LANES)
        offset = columns_ref[:, here]
        target = jnp.where(offset == halo + 1, -window, lane + offset + halo)
        for k in range(chunks):
            target_ref[k * slots : (k + 1) * slots, :] = jnp.clip(target - LANES * k, -1, LANES).astype(F32)
        values = extended_ref[:, pl.ds(first, window)]
        sums = [jnp.zeros((modes, LANES), F32) for _ in range(parts)]
        for pair in range(slots // 2):
            both = []
            for j in (2 * pair, 2 * pair + 1):
                hits = []
                for k in range(chunks):
                    row = k * slots + j
                    wanted = jnp.broadcast_to(target_ref[row : row + 1, :], (16, LANES)).astype(BF16)
                    hits += [jnp.where(i == wanted, one, zero) for i in ids]
                both.append(jnp.concatenate(hits, axis=0))
            picked = jnp.dot(values, jnp.concatenate(both, axis=1), preferred_element_type=F32)
            for side in range(2):
                j = 2 * pair + side
                for b in range(parts):
                    nearby = picked[b * modes : (b + 1) * modes, side * LANES : (side + 1) * LANES]
                    for a in range(parts):
                        row = (j * parts + a) * parts + b
                        sums[a] = sums[a] + weights_ref[row : row + 1, here] * nearby
        for a in range(parts):
            image_ref[a, :, here] = sums[a].astype(BF16)
        return carry

    lax.fori_loop(0, nodes // LANES, node_block, 0)


def stencil(columns, weights, before, basis, after):
    slots, nodes = columns.shape
    parts, modes, halo = before.shape
    return pl.pallas_call(
        stencil_kernel,
        out_shape=jax.ShapeDtypeStruct(basis.shape, BF16),
        scratch_shapes=[
            pltpu.VMEM((parts * modes, nodes + 2 * halo), BF16),
            pltpu.VMEM((slots * (LANES + 2 * halo) // LANES, LANES), F32),
        ],
        name="stencil",
    )(columns, weights, before, basis, after)


def sampled_kernel(place_ref, inverse_ref, image_ref, out_ref):
    parts, modes, nodes = image_ref.shape
    samples = place_ref.shape[1]
    total = jnp.zeros((modes, samples), F32)
    for c in range(parts):
        for first in range(0, nodes, 256):
            ids = lax.broadcasted_iota(jnp.int32, (256, samples), 0) + (c * nodes + first)
            hit = jnp.where(ids == place_ref[...], 1.0, 0.0).astype(BF16)
            total = total + jnp.dot(image_ref[c, :, first : first + 256], hit, preferred_element_type=F32)
    out_ref[...] = lax.dot_general(
        inverse_ref[...], total.astype(BF16), (((1,), (1,)), ((), ())), preferred_element_type=F32
    )


def sampled(place, inverse, image):
    return pl.pallas_call(
        sampled_kernel,
        out_shape=jax.ShapeDtypeStruct((inverse.shape[0], image.shape[1]), F32),
        name="sampled",
    )(place, inverse, image)


def reduced_kernel(core_ref, mine_ref, theirs_ref, image_ref, sampled_ref, out_ref):
    chips, parts, modes, _ = mine_ref.shape
    core = core_ref[0]
    for x in range(chips):
        for source, ref in ((core, mine_ref), (1 - core, theirs_ref)):
            total = jnp.zeros((modes, modes), F32)
            for c in range(parts):
                total = total + lax.dot_general(
                    ref[x, c], image_ref[c], (((1,), (1,)), ((), ())), preferred_element_type=F32
                )
            first = pl.multiple_of((2 * x + source) * modes, modes)
            out_ref[pl.ds(first, modes), 0:modes] = total
    out_ref[:, modes : 2 * modes] = sampled_ref[...]


def reduced_rows(core, mine, theirs, image, sampled_part):
    chips, _, modes, _ = mine.shape
    return pl.pallas_call(
        reduced_kernel,
        in_specs=[pl.BlockSpec(memory_space=pltpu.SMEM)] + [pl.BlockSpec(memory_space=pltpu.VMEM)] * 4,
        out_specs=pl.BlockSpec(memory_space=pltpu.VMEM),
        out_shape=jax.ShapeDtypeStruct((2 * chips * modes, 2 * modes), F32),
        name="reduced",
    )(core, mine, theirs, image, sampled_part)


def shards(mode_basis, blocks, columns, samples, inverse):
    parts, modes, node_count = mode_basis.shape
    halo = node_count // 4
    chips = lax.axis_size("x")
    doms = lax.axis_size(DOM)
    dom = lax.axis_index(DOM)
    up = [(i, i + 1) for i in range(doms - 1)]
    down = [(i + 1, i) for i in range(doms - 1)]
    before = lax.ppermute(mode_basis[:, :, node_count - halo :], DOM, up)
    after = lax.ppermute(mode_basis[:, :, :halo], DOM, down)
    mine = lax.all_to_all(jnp.broadcast_to(mode_basis[None], (chips, *mode_basis.shape)), "x", 0, 0)
    weights = blocks.astype(F32).reshape(-1, node_count)
    image = stencil(columns, weights, before, mode_basis, after)
    node = samples // 3 - dom * node_count
    owned = (node >= 0) & (node < node_count)
    place = jnp.where(owned, (samples % 3) * node_count + node, -1)[None]
    sampled_part = sampled(place, inverse, image)
    theirs = lax.ppermute(mine, "core", [(0, 1), (1, 0)])
    core = lax.axis_index("core").astype(jnp.int32)[None]
    partial = reduced_rows(core, mine, theirs, image, sampled_part)
    pieces = lax.all_to_all(partial.reshape(doms, -1, 2 * modes), DOM, 0, 0)
    total = jnp.sum(pieces, axis=0)
    scaling = 1.0 / math.sqrt(3 * node_count * doms)
    return total[:, :modes] * scaling, total[:, modes:]


def solution(mesh):
    mesh = Mesh(mesh.devices.reshape(4, 16, 4, 2), DOM + MODE)
    return jax.shard_map(
        shards,
        mesh=mesh,
        in_specs=(P(None, MODE, DOM), P(None, None, None, DOM), P(None, DOM), P(), P()),
        out_specs=(P(DOM, MODE), P(DOM, MODE)),
        check_vma=False,
    )
```

```python
import math

import jax
import jax.numpy as jnp
from jax import lax
from jax.experimental import pallas as pl
from jax.experimental.pallas import tpu as pltpu
from jax.sharding import Mesh, PartitionSpec as P


DOM = ("y", "z")
MODE = ("x", "core")
F32 = jnp.float32
BF16 = jnp.bfloat16
LANES = 128


def in_vmem(x):
    return pltpu.with_memory_space_constraint(x, pltpu.VMEM)


PARAMS = pltpu.CompilerParams(vmem_limit_bytes=16 * 2**20)
VMEM_SPEC = pl.BlockSpec(memory_space=pltpu.VMEM)


def spread_kernel(basis_ref, copies_ref, first_ref, last_ref):
    nodes, halo = basis_ref.shape[2], first_ref.shape[2]
    for x in range(copies_ref.shape[0]):
        copies_ref[x] = basis_ref[...]
    first_ref[...] = basis_ref[:, :, :halo]
    last_ref[...] = basis_ref[:, :, nodes - halo :]


def spread(basis, chips):
    parts, modes, nodes = basis.shape
    side = pltpu.VMEM((parts, modes, nodes // 4), BF16)
    return pl.pallas_call(
        spread_kernel,
        out_shape=(pltpu.VMEM((chips, *basis.shape), BF16), side, side),
        in_specs=[VMEM_SPEC],
        out_specs=(VMEM_SPEC,) * 3,
        compiler_params=PARAMS,
        name="spread",
    )(basis)


def slot_sums(columns_ref, blocks_ref, target_ref, weights_ref, image_ref, values, here, there, halo):
    slots = columns_ref.shape[0]
    parts, modes, _ = image_ref.shape
    window = values.shape[1]
    chunks = window // LANES
    lane = lax.broadcasted_iota(jnp.int32, (slots, LANES), 1)
    row_ids = lax.broadcasted_iota(jnp.int32, (16, LANES), 0)
    one = jnp.ones((16, LANES), BF16)
    zero = jnp.zeros((16, LANES), BF16)
    ids = [(row_ids + 16 * q).astype(F32).astype(BF16) for q in range(LANES // 16)]
    offset = columns_ref[:, here]
    target = jnp.where(offset == halo + 1, -window, lane + offset + halo)
    for k in range(chunks):
        target_ref[k * slots : (k + 1) * slots, :] = jnp.clip(target - LANES * k, -1, LANES).astype(F32)
    for a in range(parts):
        for b in range(parts):
            row = (a * parts + b) * slots
            weights_ref[row : row + slots, :] = blocks_ref[a, b, :, here].astype(F32)
    sums = [jnp.zeros((modes, LANES), F32) for _ in range(parts)]
    for pair in range(slots // 2):
        both = []
        for j in (2 * pair, 2 * pair + 1):
            hits = []
            for k in range(chunks):
                row = k * slots + j
                wanted = jnp.broadcast_to(target_ref[row : row + 1, :], (16, LANES)).astype(BF16)
                hits += [jnp.where(i == wanted, one, zero) for i in ids]
            both.append(jnp.concatenate(hits, axis=0))
        picked = jnp.dot(values, jnp.concatenate(both, axis=1), preferred_element_type=F32)
        for side in range(2):
            j = 2 * pair + side
            for b in range(parts):
                nearby = picked[b * modes : (b + 1) * modes, side * LANES : (side + 1) * LANES]
                for a in range(parts):
                    row = (a * parts + b) * slots + j
                    sums[a] = sums[a] + weights_ref[row : row + 1, :] * nearby
    for a in range(parts):
        image_ref[a, :, there] = sums[a].astype(BF16)


def inner_kernel(columns_ref, blocks_ref, basis_ref, image_ref, target_ref, weights_ref):
    parts, modes, nodes = basis_ref.shape
    halo = nodes // 4
    window = LANES + 2 * halo

    def node_block(step, carry):
        first = pl.multiple_of(step * LANES, LANES)
        values = basis_ref[:, :, pl.ds(first, window)].reshape(parts * modes, window)
        here = pl.ds(pl.multiple_of(first + halo, LANES), LANES)
        slot_sums(columns_ref, blocks_ref, target_ref, weights_ref, image_ref, values, here, pl.ds(first, LANES), halo)
        return carry

    lax.fori_loop(0, (nodes - 2 * halo) // LANES, node_block, 0)


def edge_kernel(
    columns_ref, blocks_ref, before_ref, basis_ref, after_ref, inner_ref, image_ref, target_ref, weights_ref, extended_ref
):
    parts, modes, nodes = basis_ref.shape
    halo = nodes // 4
    window = LANES + 2 * halo
    for b in range(parts):
        rows = slice(b * modes, (b + 1) * modes)
        extended_ref[0, rows, 0:halo] = before_ref[b]
        extended_ref[0, rows, halo:] = basis_ref[b, :, : 2 * halo]
        extended_ref[1, rows, : 2 * halo] = basis_ref[b, :, nodes - 2 * halo :]
        extended_ref[1, rows, 2 * halo :] = after_ref[b]
        image_ref[b, :, halo : nodes - halo] = inner_ref[b]
    blocks = halo // LANES

    def node_block(step, carry):
        side = step // blocks
        local = pl.multiple_of((step % blocks) * LANES, LANES)
        values = extended_ref[side, :, pl.ds(local, window)]
        here = pl.ds(pl.multiple_of(local + side * (nodes - halo), LANES), LANES)
        slot_sums(columns_ref, blocks_ref, target_ref, weights_ref, image_ref, values, here, here, halo)
        return carry

    lax.fori_loop(0, 2 * blocks, node_block, 0)


def slot_scratch(slots, parts, halo):
    return [
        pltpu.VMEM((slots * (LANES + 2 * halo) // LANES, LANES), F32),
        pltpu.VMEM((parts * parts * slots, LANES), F32),
    ]


def cost(flops, nbytes):
    return pl.CostEstimate(flops=flops, transcendentals=0, bytes_accessed=nbytes)


def inner(columns, blocks, basis):
    slots, nodes = columns.shape
    parts, modes, _ = basis.shape
    return pl.pallas_call(
        inner_kernel,
        out_shape=pltpu.VMEM((parts, modes, nodes // 2), BF16),
        in_specs=[VMEM_SPEC] * 3,
        out_specs=VMEM_SPEC,
        scratch_shapes=slot_scratch(slots, parts, nodes // 4),
        cost_estimate=cost(4 * 10**9, 2 * 10**6),
        compiler_params=PARAMS,
        name="inner",
    )(columns, blocks, in_vmem(basis))


def edges(columns, blocks, before, basis, after, inner_image):
    slots, _ = columns.shape
    parts, modes, halo = before.shape
    return pl.pallas_call(
        edge_kernel,
        out_shape=pltpu.VMEM(basis.shape, BF16),
        out_specs=VMEM_SPEC,
        scratch_shapes=slot_scratch(slots, parts, halo) + [pltpu.VMEM((2, parts * modes, 3 * halo), BF16)],
        cost_estimate=cost(4 * 10**9, 2 * 10**6),
        in_specs=[VMEM_SPEC] * 6,
        compiler_params=PARAMS,
        name="edges",
    )(columns, blocks, in_vmem(before), in_vmem(basis), in_vmem(after), in_vmem(inner_image))


def sampled_kernel(place_ref, inverse_ref, image_ref, out_ref):
    parts, modes, nodes = image_ref.shape
    samples = place_ref.shape[1]
    row_ids = lax.broadcasted_iota(jnp.int32, (16, samples), 0)
    one = jnp.ones((16, samples), BF16)
    zero = jnp.zeros((16, samples), BF16)
    ids = [(row_ids + 16 * q).astype(F32).astype(BF16) for q in range(LANES // 16)]
    place = jnp.broadcast_to(place_ref[...], (16, samples))
    total = jnp.zeros((modes, samples), F32)
    for c in range(parts):
        hits = []
        for first in range(0, nodes, LANES):
            wanted = jnp.clip(place - (c * nodes + first), -1, LANES).astype(F32).astype(BF16)
            hits += [jnp.where(i == wanted, one, zero) for i in ids]
        total = total + jnp.dot(image_ref[c], jnp.concatenate(hits, axis=0), preferred_element_type=F32)
    out_ref[:, 0:modes] = jnp.zeros((inverse_ref.shape[0], modes), F32)
    out_ref[:, modes:] = lax.dot_general(
        inverse_ref[...], total.astype(BF16), (((1,), (1,)), ((), ())), preferred_element_type=F32
    )


def sampled(place, inverse, image):
    return pl.pallas_call(
        sampled_kernel,
        in_specs=[VMEM_SPEC] * 3,
        out_shape=jax.ShapeDtypeStruct((inverse.shape[0], 2 * image.shape[1]), F32),
        cost_estimate=cost(2 * 10**9, 2 * 10**6),
        compiler_params=PARAMS,
        name="sampled",
    )(place, inverse, in_vmem(image))


def reduced_kernel(core_ref, basis_ref, image_ref, rest_ref, out_ref):
    chips, parts, modes, nodes = basis_ref.shape
    out_ref[...] = rest_ref[...]
    total = jnp.zeros((chips * modes, modes), F32)
    for c in range(parts):
        total = total + lax.dot_general(
            basis_ref[:, c].reshape(chips * modes, nodes), image_ref[c], (((1,), (1,)), ((), ())), preferred_element_type=F32
        )
    for x in range(chips):
        first = pl.multiple_of((2 * x + core_ref[0]) * modes, modes)
        out_ref[pl.ds(first, modes), 0:modes] = total[x * modes : (x + 1) * modes]


def reduced_rows(core, basis, image, rest):
    return pl.pallas_call(
        reduced_kernel,
        in_specs=[pl.BlockSpec(memory_space=pltpu.SMEM)] + [VMEM_SPEC] * 3,
        out_specs=VMEM_SPEC,
        out_shape=pltpu.VMEM(rest.shape, F32),
        cost_estimate=cost(2 * 10**9, 2 * 10**6),
        compiler_params=PARAMS,
        name="reduced",
    )(core, in_vmem(basis), in_vmem(image), rest)


def shards(mode_basis, blocks, columns, samples, inverse):
    parts, modes, node_count = mode_basis.shape
    chips = lax.axis_size("x")
    doms = lax.axis_size(DOM)
    dom = lax.axis_index(DOM)
    copies, first, last = spread(mode_basis, chips)
    mine = lax.all_to_all(copies, "x", 0, 0)
    before = lax.ppermute(last, DOM, [(i, (i + 1) % doms) for i in range(doms)])
    after = lax.ppermute(first, DOM, [((i + 1) % doms, i) for i in range(doms)])
    blocks = jnp.transpose(blocks, (1, 2, 0, 3))
    inner_image = inner(columns, blocks, mode_basis)
    image = edges(columns, blocks, before, mode_basis, after, inner_image)
    node = samples // 3 - dom * node_count
    owned = (node >= 0) & (node < node_count)
    place = jnp.where(owned, (samples % 3) * node_count + node, -1)[None]
    theirs = lax.ppermute(mine, "core", [(0, 1), (1, 0)])
    partial = sampled(place, inverse, image)
    core = lax.axis_index("core").astype(jnp.int32)[None]
    partial = reduced_rows(core, mine, image, partial)
    partial = reduced_rows(1 - core, theirs, image, in_vmem(partial))
    pieces = lax.all_to_all(partial.reshape(doms, -1, 2 * modes), DOM, 0, 0)
    total = jnp.sum(pieces, axis=0)
    scaling = 1.0 / math.sqrt(parts * node_count * doms)
    return total[:, :modes] * scaling, total[:, modes:]


def solution(mesh):
    step_mesh = Mesh(mesh.devices.reshape(4, 16, 4, 2), DOM + MODE)

    return jax.shard_map(
        shards,
        mesh=step_mesh,
        in_specs=(P(None, MODE, DOM), P(None, None, None, DOM), P(None, DOM), P(), P()),
        out_specs=(P(DOM, MODE), P(DOM, MODE)),
        check_vma=False,
    )
```

```python
import functools
import math

import jax
import jax.numpy as jnp
from jax import lax
from jax.experimental import pallas as pl
from jax.experimental.pallas import tpu as pltpu
from jax.sharding import Mesh, PartitionSpec as P


DOM = ("y", "z")
MODE = ("x", "core")
F32 = jnp.float32
BF16 = jnp.bfloat16
LANES = 128
TRAVEL = BF16


def in_vmem(x):
    return pltpu.with_memory_space_constraint(x, pltpu.VMEM)


PARAMS = pltpu.CompilerParams(vmem_limit_bytes=16 * 2**20)
VMEM_SPEC = pl.BlockSpec(memory_space=pltpu.VMEM)


def spread_kernel(basis_ref, copies_ref, first_ref, last_ref):
    nodes, halo = basis_ref.shape[2], first_ref.shape[2]
    for x in range(copies_ref.shape[0]):
        copies_ref[x] = basis_ref[...]
    first_ref[...] = basis_ref[:, :, :halo]
    last_ref[...] = basis_ref[:, :, nodes - halo :]


def spread(basis, chips):
    parts, modes, nodes = basis.shape
    side = pltpu.VMEM((parts, modes, nodes // 4), BF16)
    return pl.pallas_call(
        spread_kernel,
        out_shape=(pltpu.VMEM((chips, *basis.shape), BF16), side, side),
        in_specs=[VMEM_SPEC],
        out_specs=(VMEM_SPEC,) * 3,
        compiler_params=PARAMS,
        name="spread",
    )(basis)


def slot_sums(columns_ref, blocks_ref, target_ref, weights_ref, image_ref, values, here, there, halo):
    slots = columns_ref.shape[0]
    parts, modes, _ = image_ref.shape
    window = values.shape[1]
    chunks = window // LANES
    lane = lax.broadcasted_iota(jnp.int32, (slots, LANES), 1)
    row_ids = lax.broadcasted_iota(jnp.int32, (16, LANES), 0)
    one = jnp.ones((16, LANES), BF16)
    zero = jnp.zeros((16, LANES), BF16)
    ids = [(row_ids + 16 * q).astype(F32).astype(BF16) for q in range(LANES // 16)]
    offset = columns_ref[:, here]
    target = jnp.where(offset == halo + 1, -LANES, lane + offset + halo)
    target_ref[:slots, :] = (target & (LANES - 1)).astype(F32)
    target_ref[slots:, :] = (target >> (LANES.bit_length() - 1)).astype(F32)
    for a in range(parts):
        for b in range(parts):
            row = (a * parts + b) * slots
            weights_ref[row : row + slots, :] = blocks_ref[a, b, :, here].astype(F32)
    sums = [jnp.zeros((modes, LANES), F32) for _ in range(parts)]
    for pair in range(slots // 2):
        both = []
        for j in (2 * pair, 2 * pair + 1):
            lower = jnp.broadcast_to(target_ref[j : j + 1, :], (16, LANES)).astype(BF16)
            upper = jnp.broadcast_to(target_ref[slots + j : slots + j + 1, :], (16, LANES)).astype(BF16)
            ones = [jnp.where(i == lower, one, zero) for i in ids]
            hits = []
            for k in range(chunks):
                inside = upper == jnp.full((16, LANES), k, BF16)
                hits += [jnp.where(inside, hit, zero) for hit in ones]
            both.append(jnp.concatenate(hits, axis=0))
        picked = jnp.dot(values, jnp.concatenate(both, axis=1), preferred_element_type=F32)
        for side in range(2):
            j = 2 * pair + side
            for b in range(parts):
                nearby = picked[b * modes : (b + 1) * modes, side * LANES : (side + 1) * LANES]
                for a in range(parts):
                    row = (a * parts + b) * slots + j
                    sums[a] = sums[a] + weights_ref[row : row + 1, :] * nearby
    for a in range(parts):
        image_ref[a, :, there] = sums[a].astype(BF16)


def inner_kernel(columns_ref, blocks_ref, basis_ref, image_ref, target_ref, weights_ref):
    parts, modes, nodes = basis_ref.shape
    halo = nodes // 4
    window = LANES + 2 * halo

    def node_blocks(step, carry):
        for k in range(2):
            first = pl.multiple_of((2 * step + k) * LANES, LANES)
            values = basis_ref[:, :, pl.ds(first, window)].reshape(parts * modes, window)
            here = pl.ds(pl.multiple_of(first + halo, LANES), LANES)
            scratch = (target_ref.at[k], weights_ref.at[k])
            slot_sums(columns_ref, blocks_ref, *scratch, image_ref, values, here, pl.ds(first, LANES), halo)
        return carry

    lax.fori_loop(0, (nodes - 2 * halo) // (2 * LANES), node_blocks, 0)


def edge_kernel(
    columns_ref, blocks_ref, before_ref, basis_ref, after_ref, inner_ref, image_ref, target_ref, weights_ref, extended_ref
):
    parts, modes, nodes = basis_ref.shape
    halo = nodes // 4
    window = LANES + 2 * halo
    for b in range(parts):
        rows = slice(b * modes, (b + 1) * modes)
        extended_ref[0, rows, 0:halo] = before_ref[b]
        extended_ref[0, rows, halo:] = basis_ref[b, :, : 2 * halo]
        extended_ref[1, rows, : 2 * halo] = basis_ref[b, :, nodes - 2 * halo :]
        extended_ref[1, rows, 2 * halo :] = after_ref[b]
        image_ref[b, :, halo : nodes - halo] = inner_ref[b]

    def node_blocks(step, carry):
        local = pl.multiple_of(step * LANES, LANES)
        for side in range(2):
            values = extended_ref[side, :, pl.ds(local, window)]
            here = pl.ds(pl.multiple_of(local + side * (nodes - halo), LANES), LANES)
            scratch = (target_ref.at[side], weights_ref.at[side])
            slot_sums(columns_ref, blocks_ref, *scratch, image_ref, values, here, here, halo)
        return carry

    lax.fori_loop(0, halo // LANES, node_blocks, 0)


def slot_scratch(slots, parts):
    return [
        pltpu.VMEM((2, 2 * slots, LANES), F32),
        pltpu.VMEM((2, parts * parts * slots, LANES), F32),
    ]


def cost(flops, nbytes):
    return pl.CostEstimate(flops=flops, transcendentals=0, bytes_accessed=nbytes)


def inner(columns, blocks, basis):
    slots, nodes = columns.shape
    parts, modes, _ = basis.shape
    return pl.pallas_call(
        inner_kernel,
        out_shape=pltpu.VMEM((parts, modes, nodes // 2), BF16),
        in_specs=[VMEM_SPEC] * 3,
        out_specs=VMEM_SPEC,
        scratch_shapes=slot_scratch(slots, parts),
        cost_estimate=cost(4 * 10**9, 2 * 10**6),
        compiler_params=PARAMS,
        name="inner",
    )(columns, blocks, in_vmem(basis))


def edges(columns, blocks, before, basis, after, inner_image):
    slots, _ = columns.shape
    parts, modes, halo = before.shape
    return pl.pallas_call(
        edge_kernel,
        out_shape=pltpu.VMEM(basis.shape, BF16),
        out_specs=VMEM_SPEC,
        scratch_shapes=slot_scratch(slots, parts) + [pltpu.VMEM((2, parts * modes, 3 * halo), BF16)],
        cost_estimate=cost(4 * 10**9, 2 * 10**6),
        in_specs=[VMEM_SPEC] * 6,
        compiler_params=PARAMS,
        name="edges",
    )(columns, blocks, in_vmem(before), in_vmem(basis), in_vmem(after), in_vmem(inner_image))


def sampled_kernel(place_ref, inverse_ref, image_ref, out_ref):
    parts, modes, nodes = image_ref.shape
    samples = place_ref.shape[1]
    row_ids = lax.broadcasted_iota(jnp.int32, (16, samples), 0)
    one = jnp.ones((16, samples), BF16)
    zero = jnp.zeros((16, samples), BF16)
    ids = [(row_ids + 16 * q).astype(F32).astype(BF16) for q in range(LANES // 16)]
    place = jnp.broadcast_to(place_ref[...], (16, samples))
    total = jnp.zeros((modes, samples), F32)
    for c in range(parts):
        hits = []
        for first in range(0, nodes, LANES):
            wanted = jnp.clip(place - (c * nodes + first), -1, LANES).astype(F32).astype(BF16)
            hits += [jnp.where(i == wanted, one, zero) for i in ids]
        total = total + jnp.dot(image_ref[c], jnp.concatenate(hits, axis=0), preferred_element_type=F32)
    out_ref[...] = lax.dot_general(
        inverse_ref[...], total.astype(BF16), (((1,), (1,)), ((), ())), preferred_element_type=F32
    )


def sampled(place, inverse, image):
    return pl.pallas_call(
        sampled_kernel,
        in_specs=[VMEM_SPEC] * 3,
        out_shape=pltpu.VMEM((inverse.shape[0], image.shape[1]), F32),
        out_specs=VMEM_SPEC,
        cost_estimate=cost(2 * 10**9, 2 * 10**6),
        compiler_params=PARAMS,
        name="sampled",
    )(place, inverse, in_vmem(image))


def reduced_kernel(basis_ref, mine_ref, theirs_ref, kept_ref, sent_ref):
    chips, parts, modes, nodes = basis_ref.shape
    for image_ref, out_ref in ((mine_ref, kept_ref), (theirs_ref, sent_ref)):
        total = jnp.zeros((chips * modes, modes), F32)
        for c in range(parts):
            rows = basis_ref[:, c].reshape(chips * modes, nodes)
            total = total + lax.dot_general(rows, image_ref[c], (((1,), (1,)), ((), ())), preferred_element_type=F32)
        out_ref[...] = total


def reduced_rows(basis, mine, theirs):
    chips, _, modes, _ = basis.shape
    out = pltpu.VMEM((chips * modes, modes), F32)
    return pl.pallas_call(
        reduced_kernel,
        in_specs=[VMEM_SPEC] * 3,
        out_shape=(out, out),
        out_specs=(VMEM_SPEC, VMEM_SPEC),
        cost_estimate=cost(2 * 10**9, 2 * 10**6),
        compiler_params=PARAMS,
        name="reduced",
    )(in_vmem(basis), in_vmem(mine), in_vmem(theirs))


def joined_kernel(core_ref, kept_ref, received_ref, sampled_ref, out_ref):
    modes = kept_ref.shape[1]
    core = core_ref[0]
    for x in range(kept_ref.shape[0] // modes):
        rows = slice(x * modes, (x + 1) * modes)
        for source, left in ((core, kept_ref[rows, :]), (1 - core, received_ref[1 - core, rows, :])):
            first = pl.multiple_of((2 * x + source) * modes, modes)
            right = sampled_ref[pl.ds(first, modes), :]
            out_ref[pl.ds(first, modes), :] = jnp.concatenate([left, right], axis=1).astype(out_ref.dtype)


def joined(core, kept, received, sampled_part):
    rows, modes = sampled_part.shape
    return pl.pallas_call(
        joined_kernel,
        in_specs=[pl.BlockSpec(memory_space=pltpu.SMEM)] + [VMEM_SPEC] * 3,
        out_shape=pltpu.VMEM((rows, 2 * modes), TRAVEL),
        out_specs=VMEM_SPEC,
        compiler_params=PARAMS,
        name="joined",
    )(core, in_vmem(kept), in_vmem(received), in_vmem(sampled_part))


def total_kernel(scaling, pieces_ref, reduced_ref, coefficients_ref):
    modes = reduced_ref.shape[1]
    total = jnp.sum(pieces_ref[...].astype(F32), axis=0)
    reduced_ref[...] = total[:, :modes] * scaling
    coefficients_ref[...] = total[:, modes:]


def totals(pieces, scaling):
    _, rows, columns = pieces.shape
    out = jax.ShapeDtypeStruct((rows, columns // 2), F32)
    return pl.pallas_call(
        functools.partial(total_kernel, scaling),
        in_specs=[VMEM_SPEC],
        out_shape=(out, out),
        out_specs=(VMEM_SPEC, VMEM_SPEC),
        compiler_params=PARAMS,
        name="totals",
    )(in_vmem(pieces))


def shards(mode_basis, blocks, columns, samples, inverse):
    parts, modes, node_count = mode_basis.shape
    chips = lax.axis_size("x")
    doms = lax.axis_size(DOM)
    dom = lax.axis_index(DOM)
    copies, first, last = spread(mode_basis, chips)
    mine = lax.all_to_all(copies, "x", 0, 0)
    before = lax.ppermute(last, DOM, [(i, (i + 1) % doms) for i in range(doms)])
    after = lax.ppermute(first, DOM, [((i + 1) % doms, i) for i in range(doms)])
    blocks = jnp.transpose(blocks, (1, 2, 0, 3))
    inner_image = inner(columns, blocks, mode_basis)
    image = edges(columns, blocks, before, mode_basis, after, inner_image)
    node = samples // 3 - dom * node_count
    owned = (node >= 0) & (node < node_count)
    place = jnp.where(owned, (samples % 3) * node_count + node, -1)[None]
    pair = [(0, 1), (1, 0)]
    other_image = lax.ppermute(image, "core", pair)
    sampled_part = sampled(place, inverse, image)
    core = lax.axis_index("core").astype(jnp.int32)[None]
    kept, sent = reduced_rows(mine, image, other_image)
    received = lax.all_gather(sent, "core")
    partial = joined(core, kept, received, sampled_part)
    pieces = lax.all_to_all(partial.reshape(doms, -1, 2 * modes), DOM, 0, 0)
    return totals(pieces, 1.0 / math.sqrt(parts * node_count * doms))


def solution(mesh):
    step_mesh = Mesh(mesh.devices.reshape(4, 16, 4, 2), DOM + MODE)

    return jax.shard_map(
        shards,
        mesh=step_mesh,
        in_specs=(P(None, MODE, DOM), P(None, None, None, DOM), P(None, DOM), P(), P()),
        out_specs=(P(DOM, MODE), P(DOM, MODE)),
        check_vma=False,
    )
```

```python
import functools
import math

import jax
import jax.numpy as jnp
from jax import lax
from jax.experimental import pallas as pl
from jax.experimental.pallas import tpu as pltpu
from jax.sharding import Mesh, PartitionSpec as P


DOM = ("y", "z")
MODE = ("x", "core")
F32 = jnp.float32
BF16 = jnp.bfloat16
LANES = 128
TRAVEL = BF16


def in_vmem(x):
    return pltpu.with_memory_space_constraint(x, pltpu.VMEM)


PARAMS = pltpu.CompilerParams(vmem_limit_bytes=16 * 2**20)
VMEM_SPEC = pl.BlockSpec(memory_space=pltpu.VMEM)


def spread_kernel(basis_ref, copies_ref, first_ref, last_ref):
    nodes, halo = basis_ref.shape[2], first_ref.shape[2]
    for x in range(copies_ref.shape[0]):
        copies_ref[x] = basis_ref[...]
    first_ref[...] = basis_ref[:, :, :halo]
    last_ref[...] = basis_ref[:, :, nodes - halo :]


def spread(basis, chips):
    parts, modes, nodes = basis.shape
    side = pltpu.VMEM((parts, modes, nodes // 4), BF16)
    return pl.pallas_call(
        spread_kernel,
        out_shape=(pltpu.VMEM((chips, *basis.shape), BF16), side, side),
        in_specs=[VMEM_SPEC],
        out_specs=(VMEM_SPEC,) * 3,
        compiler_params=PARAMS,
        name="spread",
    )(basis)


def slot_sums(columns_ref, blocks_ref, target_ref, weights_ref, image_ref, values, here, there, halo):
    slots = columns_ref.shape[0]
    parts, modes, _ = image_ref.shape
    window = values.shape[1]
    chunks = window // LANES
    lane = lax.broadcasted_iota(jnp.int32, (slots, LANES), 1)
    row_ids = lax.broadcasted_iota(jnp.int32, (16, LANES), 0)
    one = jnp.ones((16, LANES), BF16)
    zero = jnp.zeros((16, LANES), BF16)
    ids = [(row_ids + 16 * q).astype(F32).astype(BF16) for q in range(LANES // 16)]
    offset = columns_ref[:, here]
    target = jnp.where(offset == halo + 1, -LANES, lane + offset + halo)
    target_ref[:slots, :] = (target & (LANES - 1)).astype(F32)
    target_ref[slots:, :] = (target >> (LANES.bit_length() - 1)).astype(F32)
    for a in range(parts):
        for b in range(parts):
            row = (a * parts + b) * slots
            weights_ref[row : row + slots, :] = blocks_ref[a, b, :, here].astype(F32)
    sums = [jnp.zeros((modes, LANES), F32) for _ in range(parts)]
    for pair in range(slots // 2):
        both = []
        for j in (2 * pair, 2 * pair + 1):
            lower = jnp.broadcast_to(target_ref[j : j + 1, :], (16, LANES)).astype(BF16)
            upper = jnp.broadcast_to(target_ref[slots + j : slots + j + 1, :], (16, LANES)).astype(BF16)
            ones = [jnp.where(i == lower, one, zero) for i in ids]
            hits = []
            for k in range(chunks):
                inside = upper == jnp.full((16, LANES), k, BF16)
                hits += [jnp.where(inside, hit, zero) for hit in ones]
            both.append(jnp.concatenate(hits, axis=0))
        picked = jnp.dot(values, jnp.concatenate(both, axis=1), preferred_element_type=F32)
        for side in range(2):
            j = 2 * pair + side
            for b in range(parts):
                nearby = picked[b * modes : (b + 1) * modes, side * LANES : (side + 1) * LANES]
                for a in range(parts):
                    row = (a * parts + b) * slots + j
                    sums[a] = sums[a] + weights_ref[row : row + 1, :] * nearby
    for a in range(parts):
        image_ref[a, :, there] = sums[a].astype(BF16)


def inner_kernel(columns_ref, blocks_ref, basis_ref, image_ref, target_ref, weights_ref):
    parts, modes, nodes = basis_ref.shape
    halo = nodes // 4
    window = LANES + 2 * halo

    def node_blocks(step, carry):
        for k in range(2):
            first = pl.multiple_of((2 * step + k) * LANES, LANES)
            values = basis_ref[:, :, pl.ds(first, window)].reshape(parts * modes, window)
            here = pl.ds(pl.multiple_of(first + halo, LANES), LANES)
            scratch = (target_ref.at[k], weights_ref.at[k])
            slot_sums(columns_ref, blocks_ref, *scratch, image_ref, values, here, pl.ds(first, LANES), halo)
        return carry

    lax.fori_loop(0, (nodes - 2 * halo) // (2 * LANES), node_blocks, 0)


def left_kernel(columns_ref, blocks_ref, before_ref, basis_ref, image_ref, target_ref, weights_ref, extended_ref):
    parts, modes, halo = before_ref.shape
    for b in range(parts):
        rows = slice(b * modes, (b + 1) * modes)
        extended_ref[rows, :halo] = before_ref[b]
        extended_ref[rows, halo:] = basis_ref[b, :, : 2 * halo]
    for k in range(halo // LANES):
        here = slice(k * LANES, (k + 1) * LANES)
        values = extended_ref[:, k * LANES : (k + 1) * LANES + 2 * halo]
        scratch = (target_ref.at[k], weights_ref.at[k])
        slot_sums(columns_ref, blocks_ref, *scratch, image_ref, values, here, here, halo)


def right_kernel(
    columns_ref, blocks_ref, after_ref, basis_ref, left_ref, inner_ref, image_ref, target_ref, weights_ref, extended_ref
):
    parts, modes, halo = after_ref.shape
    nodes = basis_ref.shape[2]
    for b in range(parts):
        rows = slice(b * modes, (b + 1) * modes)
        extended_ref[rows, : 2 * halo] = basis_ref[b, :, nodes - 2 * halo :]
        extended_ref[rows, 2 * halo :] = after_ref[b]
        image_ref[b, :, :halo] = left_ref[b]
        image_ref[b, :, halo : nodes - halo] = inner_ref[b]
    for k in range(halo // LANES):
        first = nodes - halo + k * LANES
        here = slice(first, first + LANES)
        values = extended_ref[:, k * LANES : (k + 1) * LANES + 2 * halo]
        scratch = (target_ref.at[k], weights_ref.at[k])
        slot_sums(columns_ref, blocks_ref, *scratch, image_ref, values, here, here, halo)


def slot_scratch(slots, parts):
    return [
        pltpu.VMEM((2, 2 * slots, LANES), F32),
        pltpu.VMEM((2, parts * parts * slots, LANES), F32),
    ]


def cost(flops, nbytes):
    return pl.CostEstimate(flops=flops, transcendentals=0, bytes_accessed=nbytes)


def inner(columns, blocks, basis):
    slots, nodes = columns.shape
    parts, modes, _ = basis.shape
    return pl.pallas_call(
        inner_kernel,
        out_shape=pltpu.VMEM((parts, modes, nodes // 2), BF16),
        in_specs=[VMEM_SPEC] * 3,
        out_specs=VMEM_SPEC,
        scratch_shapes=slot_scratch(slots, parts),
        cost_estimate=cost(4 * 10**9, 2 * 10**6),
        compiler_params=PARAMS,
        name="inner",
    )(columns, blocks, in_vmem(basis))


def edge(kernel, columns, blocks, reached, basis, others, image_nodes):
    slots, _ = columns.shape
    parts, modes, halo = reached.shape
    return pl.pallas_call(
        kernel,
        out_shape=pltpu.VMEM((parts, modes, image_nodes), BF16),
        in_specs=[VMEM_SPEC] * (4 + len(others)),
        out_specs=VMEM_SPEC,
        scratch_shapes=slot_scratch(slots, parts) + [pltpu.VMEM((parts * modes, 3 * halo), BF16)],
        cost_estimate=cost(2 * 10**9, 10**6),
        compiler_params=PARAMS,
    )(columns, blocks, in_vmem(reached), in_vmem(basis), *(in_vmem(x) for x in others))


def sampled_kernel(place_ref, inverse_ref, image_ref, out_ref):
    parts, modes, nodes = image_ref.shape
    samples = place_ref.shape[1]
    row_ids = lax.broadcasted_iota(jnp.int32, (16, samples), 0)
    one = jnp.ones((16, samples), BF16)
    zero = jnp.zeros((16, samples), BF16)
    ids = [(row_ids + 16 * q).astype(F32).astype(BF16) for q in range(LANES // 16)]
    place = jnp.broadcast_to(place_ref[...], (16, samples))
    total = jnp.zeros((modes, samples), F32)
    for c in range(parts):
        hits = []
        for first in range(0, nodes, LANES):
            wanted = jnp.clip(place - (c * nodes + first), -1, LANES).astype(F32).astype(BF16)
            hits += [jnp.where(i == wanted, one, zero) for i in ids]
        total = total + jnp.dot(image_ref[c], jnp.concatenate(hits, axis=0), preferred_element_type=F32)
    out_ref[...] = lax.dot_general(
        inverse_ref[...], total.astype(BF16), (((1,), (1,)), ((), ())), preferred_element_type=F32
    )


def sampled(place, inverse, image):
    return pl.pallas_call(
        sampled_kernel,
        in_specs=[VMEM_SPEC] * 3,
        out_shape=pltpu.VMEM((inverse.shape[0], image.shape[1]), F32),
        out_specs=VMEM_SPEC,
        cost_estimate=cost(2 * 10**9, 2 * 10**6),
        compiler_params=PARAMS,
        name="sampled",
    )(place, inverse, in_vmem(image))


def reduced_kernel(basis_ref, mine_ref, theirs_ref, kept_ref, sent_ref):
    chips, parts, modes, nodes = basis_ref.shape
    total = jnp.zeros((chips * modes, 2 * modes), F32)
    for c in range(parts):
        rows = basis_ref[:, c].reshape(chips * modes, nodes)
        both = jnp.concatenate([mine_ref[c], theirs_ref[c]], axis=0)
        total = total + lax.dot_general(rows, both, (((1,), (1,)), ((), ())), preferred_element_type=F32)
    kept_ref[...] = total[:, :modes]
    sent_ref[...] = total[:, modes:]


def reduced_rows(basis, mine, theirs):
    chips, _, modes, _ = basis.shape
    out = pltpu.VMEM((chips * modes, modes), F32)
    return pl.pallas_call(
        reduced_kernel,
        in_specs=[VMEM_SPEC] * 3,
        out_shape=(out, out),
        out_specs=(VMEM_SPEC, VMEM_SPEC),
        cost_estimate=cost(2 * 10**9, 2 * 10**6),
        compiler_params=PARAMS,
        name="reduced",
    )(in_vmem(basis), in_vmem(mine), in_vmem(theirs))


def joined_kernel(core_ref, kept_ref, received_ref, sampled_ref, out_ref):
    modes = kept_ref.shape[1]
    core = core_ref[0]
    for x in range(kept_ref.shape[0] // modes):
        rows = slice(x * modes, (x + 1) * modes)
        for source, left in ((core, kept_ref[rows, :]), (1 - core, received_ref[1 - core, rows, :])):
            first = pl.multiple_of((2 * x + source) * modes, modes)
            right = sampled_ref[pl.ds(first, modes), :]
            out_ref[pl.ds(first, modes), :] = jnp.concatenate([left, right], axis=1).astype(out_ref.dtype)


def joined(core, kept, received, sampled_part):
    rows, modes = sampled_part.shape
    return pl.pallas_call(
        joined_kernel,
        in_specs=[pl.BlockSpec(memory_space=pltpu.SMEM)] + [VMEM_SPEC] * 3,
        out_shape=pltpu.VMEM((rows, 2 * modes), TRAVEL),
        out_specs=VMEM_SPEC,
        compiler_params=PARAMS,
        name="joined",
    )(core, in_vmem(kept), in_vmem(received), in_vmem(sampled_part))


def total_kernel(scaling, pieces_ref, reduced_ref, coefficients_ref):
    modes = reduced_ref.shape[1]
    total = jnp.sum(pieces_ref[...].astype(F32), axis=0)
    reduced_ref[...] = total[:, :modes] * scaling
    coefficients_ref[...] = total[:, modes:]


def totals(pieces, scaling):
    _, rows, columns = pieces.shape
    out = jax.ShapeDtypeStruct((rows, columns // 2), F32)
    return pl.pallas_call(
        functools.partial(total_kernel, scaling),
        in_specs=[VMEM_SPEC],
        out_shape=(out, out),
        out_specs=(VMEM_SPEC, VMEM_SPEC),
        compiler_params=PARAMS,
        name="totals",
    )(in_vmem(pieces))


def shards(mode_basis, blocks, columns, samples, inverse):
    parts, modes, node_count = mode_basis.shape
    chips = lax.axis_size("x")
    doms = lax.axis_size(DOM)
    dom = lax.axis_index(DOM)
    copies, first, last = spread(mode_basis, chips)
    mine = lax.all_to_all(copies, "x", 0, 0)
    before = lax.ppermute(last, DOM, [(i, (i + 1) % doms) for i in range(doms)])
    after = lax.ppermute(first, DOM, [((i + 1) % doms, i) for i in range(doms)])
    blocks = jnp.transpose(blocks, (1, 2, 0, 3))
    inner_image = inner(columns, blocks, mode_basis)
    left_image = edge(left_kernel, columns, blocks, before, mode_basis, (), node_count // 4)
    others = (left_image, inner_image)
    image = edge(right_kernel, columns, blocks, after, mode_basis, others, node_count)
    node = samples // 3 - dom * node_count
    owned = (node >= 0) & (node < node_count)
    place = jnp.where(owned, (samples % 3) * node_count + node, -1)[None]
    pair = [(0, 1), (1, 0)]
    other_image = lax.ppermute(image, "core", pair)
    sampled_part = sampled(place, inverse, image)
    core = lax.axis_index("core").astype(jnp.int32)[None]
    kept, sent = reduced_rows(mine, image, other_image)
    received = lax.all_gather(sent, "core")
    partial = joined(core, kept, received, sampled_part)
    pieces = lax.all_to_all(partial.reshape(doms, -1, 2 * modes), DOM, 0, 0)
    return totals(pieces, 1.0 / math.sqrt(parts * node_count * doms))


def solution(mesh):
    step_mesh = Mesh(mesh.devices.reshape(4, 16, 4, 2), DOM + MODE)

    return jax.shard_map(
        shards,
        mesh=step_mesh,
        in_specs=(P(None, MODE, DOM), P(None, None, None, DOM), P(None, DOM), P(), P()),
        out_specs=(P(DOM, MODE), P(DOM, MODE)),
        check_vma=False,
    )
```

```python
import functools
import math

import jax
import jax.numpy as jnp
from jax import lax
from jax.experimental import pallas as pl
from jax.experimental.pallas import tpu as pltpu
from jax.sharding import Mesh, PartitionSpec as P


DOM = ("y", "z")
MODE = ("x", "core")
F32 = jnp.float32
BF16 = jnp.bfloat16
LANES = 128
TRAVEL = BF16


def in_vmem(x):
    return pltpu.with_memory_space_constraint(x, pltpu.VMEM)


PARAMS = pltpu.CompilerParams(vmem_limit_bytes=16 * 2**20)
VMEM_SPEC = pl.BlockSpec(memory_space=pltpu.VMEM)


def spread_kernel(basis_ref, copies_ref, first_ref, last_ref, sems):
    nodes, halo = basis_ref.shape[2], first_ref.shape[2]
    moves = [pltpu.make_async_copy(basis_ref, copies_ref.at[x], sems.at[x]) for x in range(copies_ref.shape[0])]
    for move in moves:
        move.start()
    first_ref[...] = basis_ref[:, :, :halo]
    last_ref[...] = basis_ref[:, :, nodes - halo :]
    for move in moves:
        move.wait()


def spread(basis, chips):
    parts, modes, nodes = basis.shape
    side = pltpu.VMEM((parts, modes, nodes // 4), BF16)
    return pl.pallas_call(
        spread_kernel,
        out_shape=(jax.ShapeDtypeStruct((chips, *basis.shape), BF16), side, side),
        in_specs=[VMEM_SPEC],
        out_specs=(pl.BlockSpec(memory_space=pltpu.HBM), VMEM_SPEC, VMEM_SPEC),
        scratch_shapes=[pltpu.SemaphoreType.DMA((chips,))],
        compiler_params=PARAMS,
        name="spread",
    )(in_vmem(basis))


def slot_sums(columns_ref, blocks_ref, target_ref, weights_ref, image_ref, values, here, there, halo):
    slots = columns_ref.shape[0]
    parts, modes, _ = image_ref.shape
    window = values.shape[1]
    chunks = window // LANES
    lane = lax.broadcasted_iota(jnp.int32, (slots, LANES), 1)
    row_ids = lax.broadcasted_iota(jnp.int32, (16, LANES), 0)
    one = jnp.ones((16, LANES), BF16)
    zero = jnp.zeros((16, LANES), BF16)
    ids = [(row_ids + 16 * q).astype(F32).astype(BF16) for q in range(LANES // 16)]
    offset = columns_ref[:, here]
    target = jnp.where(offset == halo + 1, -LANES, lane + offset + halo)
    target_ref[:slots, :] = (target & (LANES - 1)).astype(F32)
    target_ref[slots:, :] = (target >> (LANES.bit_length() - 1)).astype(F32)
    for a in range(parts):
        for b in range(parts):
            row = (a * parts + b) * slots
            weights_ref[row : row + slots, :] = blocks_ref[a, b, :, here].astype(F32)
    sums = [jnp.zeros((modes, LANES), F32) for _ in range(parts)]
    for pair in range(slots // 2):
        both = []
        for j in (2 * pair, 2 * pair + 1):
            lower = jnp.broadcast_to(target_ref[j : j + 1, :], (16, LANES)).astype(BF16)
            upper = jnp.broadcast_to(target_ref[slots + j : slots + j + 1, :], (16, LANES)).astype(BF16)
            ones = [jnp.where(i == lower, one, zero) for i in ids]
            hits = []
            for k in range(chunks):
                inside = upper == jnp.full((16, LANES), k, BF16)
                hits += [jnp.where(inside, hit, zero) for hit in ones]
            both.append(jnp.concatenate(hits, axis=0))
        picked = jnp.dot(values, jnp.concatenate(both, axis=1), preferred_element_type=F32)
        for side in range(2):
            j = 2 * pair + side
            for b in range(parts):
                nearby = picked[b * modes : (b + 1) * modes, side * LANES : (side + 1) * LANES]
                for a in range(parts):
                    row = (a * parts + b) * slots + j
                    sums[a] = sums[a] + weights_ref[row : row + 1, :] * nearby
    for a in range(parts):
        image_ref[a, :, there] = sums[a].astype(BF16)


def inner_kernel(columns_ref, blocks_ref, basis_ref, image_ref, target_ref, weights_ref):
    parts, modes, nodes = basis_ref.shape
    halo = nodes // 4
    window = LANES + 2 * halo

    def node_blocks(step, carry):
        for k in range(2):
            first = pl.multiple_of((2 * step + k) * LANES, LANES)
            values = basis_ref[:, :, pl.ds(first, window)].reshape(parts * modes, window)
            here = pl.ds(pl.multiple_of(first + halo, LANES), LANES)
            scratch = (target_ref.at[k], weights_ref.at[k])
            slot_sums(columns_ref, blocks_ref, *scratch, image_ref, values, here, pl.ds(first, LANES), halo)
        return carry

    lax.fori_loop(0, (nodes - 2 * halo) // (2 * LANES), node_blocks, 0)


def left_kernel(columns_ref, blocks_ref, before_ref, basis_ref, image_ref, target_ref, weights_ref, extended_ref):
    parts, modes, halo = before_ref.shape
    for b in range(parts):
        rows = slice(b * modes, (b + 1) * modes)
        extended_ref[rows, :halo] = before_ref[b]
        extended_ref[rows, halo:] = basis_ref[b, :, : 2 * halo]
    for k in range(halo // LANES):
        here = slice(k * LANES, (k + 1) * LANES)
        values = extended_ref[:, k * LANES : (k + 1) * LANES + 2 * halo]
        scratch = (target_ref.at[k], weights_ref.at[k])
        slot_sums(columns_ref, blocks_ref, *scratch, image_ref, values, here, here, halo)


def right_kernel(
    columns_ref, blocks_ref, after_ref, basis_ref, left_ref, inner_ref, image_ref, target_ref, weights_ref, extended_ref
):
    parts, modes, halo = after_ref.shape
    nodes = basis_ref.shape[2]
    for b in range(parts):
        rows = slice(b * modes, (b + 1) * modes)
        extended_ref[rows, : 2 * halo] = basis_ref[b, :, nodes - 2 * halo :]
        extended_ref[rows, 2 * halo :] = after_ref[b]
        image_ref[b, :, :halo] = left_ref[b]
        image_ref[b, :, halo : nodes - halo] = inner_ref[b]
    for k in range(halo // LANES):
        first = nodes - halo + k * LANES
        here = slice(first, first + LANES)
        values = extended_ref[:, k * LANES : (k + 1) * LANES + 2 * halo]
        scratch = (target_ref.at[k], weights_ref.at[k])
        slot_sums(columns_ref, blocks_ref, *scratch, image_ref, values, here, here, halo)


def slot_scratch(slots, parts):
    return [
        pltpu.VMEM((2, 2 * slots, LANES), F32),
        pltpu.VMEM((2, parts * parts * slots, LANES), F32),
    ]


def cost(flops, nbytes):
    return pl.CostEstimate(flops=flops, transcendentals=0, bytes_accessed=nbytes)


def inner(columns, blocks, basis):
    slots, nodes = columns.shape
    parts, modes, _ = basis.shape
    return pl.pallas_call(
        inner_kernel,
        out_shape=pltpu.VMEM((parts, modes, nodes // 2), BF16),
        in_specs=[VMEM_SPEC] * 3,
        out_specs=VMEM_SPEC,
        scratch_shapes=slot_scratch(slots, parts),
        cost_estimate=cost(4 * 10**9, 2 * 10**6),
        compiler_params=PARAMS,
        name="inner",
    )(columns, blocks, in_vmem(basis))


def edge(kernel, columns, blocks, reached, basis, others, image_nodes):
    slots, _ = columns.shape
    parts, modes, halo = reached.shape
    return pl.pallas_call(
        kernel,
        out_shape=pltpu.VMEM((parts, modes, image_nodes), BF16),
        in_specs=[VMEM_SPEC] * (4 + len(others)),
        out_specs=VMEM_SPEC,
        scratch_shapes=slot_scratch(slots, parts) + [pltpu.VMEM((parts * modes, 3 * halo), BF16)],
        cost_estimate=cost(2 * 10**9, 10**6),
        compiler_params=PARAMS,
    )(columns, blocks, in_vmem(reached), in_vmem(basis), *(in_vmem(x) for x in others))


def sampled_kernel(place_ref, inverse_ref, image_ref, out_ref):
    parts, modes, nodes = image_ref.shape
    samples = place_ref.shape[1]
    row_ids = lax.broadcasted_iota(jnp.int32, (16, samples), 0)
    one = jnp.ones((16, samples), BF16)
    zero = jnp.zeros((16, samples), BF16)
    ids = [(row_ids + 16 * q).astype(F32).astype(BF16) for q in range(LANES // 16)]
    place = jnp.broadcast_to(place_ref[...], (16, samples))
    total = jnp.zeros((modes, samples), F32)
    for c in range(parts):
        hits = []
        for first in range(0, nodes, LANES):
            wanted = jnp.clip(place - (c * nodes + first), -1, LANES).astype(F32).astype(BF16)
            hits += [jnp.where(i == wanted, one, zero) for i in ids]
        total = total + jnp.dot(image_ref[c], jnp.concatenate(hits, axis=0), preferred_element_type=F32)
    out_ref[...] = lax.dot_general(
        inverse_ref[...], total.astype(BF16), (((1,), (1,)), ((), ())), preferred_element_type=F32
    )


def sampled(place, inverse, image):
    return pl.pallas_call(
        sampled_kernel,
        in_specs=[VMEM_SPEC] * 3,
        out_shape=pltpu.VMEM((inverse.shape[0], image.shape[1]), F32),
        out_specs=VMEM_SPEC,
        cost_estimate=cost(2 * 10**9, 2 * 10**6),
        compiler_params=PARAMS,
        name="sampled",
    )(place, inverse, in_vmem(image))


def reduced_kernel(basis_ref, mine_ref, theirs_ref, kept_ref, sent_ref):
    chips, parts, modes, nodes = basis_ref.shape
    total = jnp.zeros((chips * modes, 2 * modes), F32)
    for c in range(parts):
        rows = basis_ref[:, c].reshape(chips * modes, nodes)
        both = jnp.concatenate([mine_ref[c], theirs_ref[c]], axis=0)
        total = total + lax.dot_general(rows, both, (((1,), (1,)), ((), ())), preferred_element_type=F32)
    kept_ref[...] = total[:, :modes]
    sent_ref[...] = total[:, modes:]


def reduced_rows(basis, mine, theirs):
    chips, _, modes, _ = basis.shape
    out = pltpu.VMEM((chips * modes, modes), F32)
    return pl.pallas_call(
        reduced_kernel,
        in_specs=[VMEM_SPEC] * 3,
        out_shape=(out, out),
        out_specs=(VMEM_SPEC, VMEM_SPEC),
        cost_estimate=cost(2 * 10**9, 2 * 10**6),
        compiler_params=PARAMS,
        name="reduced",
    )(in_vmem(basis), in_vmem(mine), in_vmem(theirs))


def joined_kernel(core_ref, kept_ref, received_ref, sampled_ref, out_ref):
    modes = kept_ref.shape[1]
    core = core_ref[0]
    for x in range(kept_ref.shape[0] // modes):
        rows = slice(x * modes, (x + 1) * modes)
        for source, left in ((core, kept_ref[rows, :]), (1 - core, received_ref[1 - core, rows, :])):
            first = pl.multiple_of((2 * x + source) * modes, modes)
            right = sampled_ref[pl.ds(first, modes), :]
            out_ref[pl.ds(first, modes), :] = jnp.concatenate([left, right], axis=1).astype(out_ref.dtype)


def joined(core, kept, received, sampled_part):
    rows, modes = sampled_part.shape
    return pl.pallas_call(
        joined_kernel,
        in_specs=[pl.BlockSpec(memory_space=pltpu.SMEM)] + [VMEM_SPEC] * 3,
        out_shape=pltpu.VMEM((rows, 2 * modes), TRAVEL),
        out_specs=VMEM_SPEC,
        compiler_params=PARAMS,
        name="joined",
    )(core, in_vmem(kept), in_vmem(received), in_vmem(sampled_part))


def total_kernel(scaling, pieces_ref, reduced_ref, coefficients_ref):
    modes = reduced_ref.shape[1]
    total = jnp.sum(pieces_ref[...].astype(F32), axis=0)
    reduced_ref[...] = total[:, :modes] * scaling
    coefficients_ref[...] = total[:, modes:]


def totals(pieces, scaling):
    _, rows, columns = pieces.shape
    out = jax.ShapeDtypeStruct((rows, columns // 2), F32)
    return pl.pallas_call(
        functools.partial(total_kernel, scaling),
        in_specs=[VMEM_SPEC],
        out_shape=(out, out),
        out_specs=(VMEM_SPEC, VMEM_SPEC),
        compiler_params=PARAMS,
        name="totals",
    )(in_vmem(pieces))


def shards(mode_basis, blocks, columns, samples, inverse):
    parts, modes, node_count = mode_basis.shape
    chips = lax.axis_size("x")
    doms = lax.axis_size(DOM)
    dom = lax.axis_index(DOM)
    copies, first, last = spread(mode_basis, chips)
    mine = lax.all_to_all(copies, "x", 0, 0)
    before = lax.ppermute(last, DOM, [(i, (i + 1) % doms) for i in range(doms)])
    after = lax.ppermute(first, DOM, [((i + 1) % doms, i) for i in range(doms)])
    blocks = jnp.transpose(blocks, (1, 2, 0, 3))
    inner_image = inner(columns, blocks, mode_basis)
    left_image = edge(left_kernel, columns, blocks, before, mode_basis, (), node_count // 4)
    others = (left_image, inner_image)
    image = edge(right_kernel, columns, blocks, after, mode_basis, others, node_count)
    node = samples // 3 - dom * node_count
    owned = (node >= 0) & (node < node_count)
    place = jnp.where(owned, (samples % 3) * node_count + node, -1)[None]
    pair = [(0, 1), (1, 0)]
    other_image = lax.ppermute(image, "core", pair)
    sampled_part = sampled(place, inverse, image)
    core = lax.axis_index("core").astype(jnp.int32)[None]
    kept, sent = reduced_rows(mine, image, other_image)
    received = lax.all_gather(sent, "core")
    partial = joined(core, kept, received, sampled_part)
    pieces = lax.all_to_all(partial.reshape(doms, -1, 2 * modes), DOM, 0, 0)
    return totals(pieces, 1.0 / math.sqrt(parts * node_count * doms))


def solution(mesh):
    step_mesh = Mesh(mesh.devices.reshape(4, 16, 4, 2), DOM + MODE)

    return jax.shard_map(
        shards,
        mesh=step_mesh,
        in_specs=(P(None, MODE, DOM), P(None, None, None, DOM), P(None, DOM), P(), P()),
        out_specs=(P(DOM, MODE), P(DOM, MODE)),
        check_vma=False,
    )
```

```python
import functools
import math

import jax
import jax.numpy as jnp
from jax import lax
from jax.experimental import pallas as pl
from jax.experimental.pallas import tpu as pltpu
from jax.sharding import Mesh, PartitionSpec as P


DOM = ("y", "z")
MODE = ("x", "core")
F32 = jnp.float32
BF16 = jnp.bfloat16
LANES = 128
TRAVEL = BF16


def in_vmem(x):
    return pltpu.with_memory_space_constraint(x, pltpu.VMEM)


PARAMS = pltpu.CompilerParams(vmem_limit_bytes=16 * 2**20)
VMEM_SPEC = pl.BlockSpec(memory_space=pltpu.VMEM)


def spread_kernel(basis_ref, copies_ref, first_ref, last_ref, sems):
    nodes, halo = basis_ref.shape[2], first_ref.shape[2]
    moves = [pltpu.make_async_copy(basis_ref, copies_ref.at[x], sems.at[x]) for x in range(copies_ref.shape[0])]
    for move in moves:
        move.start()
    first_ref[...] = basis_ref[:, :, :halo]
    last_ref[...] = basis_ref[:, :, nodes - halo :]
    for move in moves:
        move.wait()


def spread(basis, chips):
    parts, modes, nodes = basis.shape
    side = pltpu.VMEM((parts, modes, nodes // 4), BF16)
    return pl.pallas_call(
        spread_kernel,
        out_shape=(jax.ShapeDtypeStruct((chips, *basis.shape), BF16), side, side),
        in_specs=[VMEM_SPEC],
        out_specs=(pl.BlockSpec(memory_space=pltpu.HBM), VMEM_SPEC, VMEM_SPEC),
        scratch_shapes=[pltpu.SemaphoreType.DMA((chips,))],
        compiler_params=PARAMS,
        name="spread",
    )(in_vmem(basis))


def slot_sums(columns_ref, blocks_ref, target_ref, weights_ref, image_ref, values, here, there, halo):
    slots = columns_ref.shape[0]
    parts, modes, _ = image_ref.shape
    window = values.shape[1]
    chunks = window // LANES
    lane = lax.broadcasted_iota(jnp.int32, (slots, LANES), 1)
    row_ids = lax.broadcasted_iota(jnp.int32, (16, LANES), 0)
    one = jnp.ones((16, LANES), BF16)
    zero = jnp.zeros((16, LANES), BF16)
    ids = [(row_ids + 16 * q).astype(F32).astype(BF16) for q in range(LANES // 16)]
    offset = columns_ref[:, here]
    target = jnp.where(offset == halo + 1, -LANES, lane + offset + halo)
    target_ref[:slots, :] = (target & (LANES - 1)).astype(F32)
    target_ref[slots:, :] = (target >> (LANES.bit_length() - 1)).astype(F32)
    for a in range(parts):
        for b in range(parts):
            row = (a * parts + b) * slots
            weights_ref[row : row + slots, :] = blocks_ref[a, b, :, here].astype(F32)
    sums = [jnp.zeros((modes, LANES), F32) for _ in range(parts)]
    for pair in range(slots // 2):
        both = []
        for j in (2 * pair, 2 * pair + 1):
            lower = jnp.broadcast_to(target_ref[j : j + 1, :], (16, LANES)).astype(BF16)
            upper = jnp.broadcast_to(target_ref[slots + j : slots + j + 1, :], (16, LANES)).astype(BF16)
            ones = [jnp.where(i == lower, one, zero) for i in ids]
            hits = []
            for k in range(chunks):
                inside = upper == jnp.full((16, LANES), k, BF16)
                hits += [jnp.where(inside, hit, zero) for hit in ones]
            both.append(jnp.concatenate(hits, axis=0))
        picked = jnp.dot(values, jnp.concatenate(both, axis=1), preferred_element_type=F32)
        for side in range(2):
            j = 2 * pair + side
            for b in range(parts):
                nearby = picked[b * modes : (b + 1) * modes, side * LANES : (side + 1) * LANES]
                for a in range(parts):
                    row = (a * parts + b) * slots + j
                    sums[a] = sums[a] + weights_ref[row : row + 1, :] * nearby
    for a in range(parts):
        image_ref[a, :, there] = sums[a].astype(BF16)


def inner_kernel(columns_ref, blocks_ref, basis_ref, image_ref, target_ref, weights_ref):
    parts, modes, nodes = basis_ref.shape
    halo = nodes // 4
    window = LANES + 2 * halo

    def node_blocks(step, carry):
        for k in range(2):
            first = pl.multiple_of((2 * step + k) * LANES, LANES)
            values = basis_ref[:, :, pl.ds(first, window)].reshape(parts * modes, window)
            here = pl.ds(pl.multiple_of(first + halo, LANES), LANES)
            scratch = (target_ref.at[k], weights_ref.at[k])
            slot_sums(columns_ref, blocks_ref, *scratch, image_ref, values, here, pl.ds(first, LANES), halo)
        return carry

    lax.fori_loop(0, (nodes - 2 * halo) // (2 * LANES), node_blocks, 0)


def left_kernel(columns_ref, blocks_ref, before_ref, basis_ref, image_ref, target_ref, weights_ref, extended_ref):
    parts, modes, halo = before_ref.shape
    for b in range(parts):
        rows = slice(b * modes, (b + 1) * modes)
        extended_ref[rows, :halo] = before_ref[b]
        extended_ref[rows, halo:] = basis_ref[b, :, : 2 * halo]
    for k in range(halo // LANES):
        here = slice(k * LANES, (k + 1) * LANES)
        values = extended_ref[:, k * LANES : (k + 1) * LANES + 2 * halo]
        scratch = (target_ref.at[k], weights_ref.at[k])
        slot_sums(columns_ref, blocks_ref, *scratch, image_ref, values, here, here, halo)


def right_kernel(
    columns_ref, blocks_ref, after_ref, basis_ref, left_ref, inner_ref, image_ref, target_ref, weights_ref, extended_ref
):
    parts, modes, halo = after_ref.shape
    nodes = basis_ref.shape[2]
    for b in range(parts):
        rows = slice(b * modes, (b + 1) * modes)
        extended_ref[rows, : 2 * halo] = basis_ref[b, :, nodes - 2 * halo :]
        extended_ref[rows, 2 * halo :] = after_ref[b]
        image_ref[b, :, :halo] = left_ref[b]
        image_ref[b, :, halo : nodes - halo] = inner_ref[b]
    for k in range(halo // LANES):
        first = nodes - halo + k * LANES
        here = slice(first, first + LANES)
        values = extended_ref[:, k * LANES : (k + 1) * LANES + 2 * halo]
        scratch = (target_ref.at[k], weights_ref.at[k])
        slot_sums(columns_ref, blocks_ref, *scratch, image_ref, values, here, here, halo)


def slot_scratch(slots, parts):
    return [
        pltpu.VMEM((2, 2 * slots, LANES), F32),
        pltpu.VMEM((2, parts * parts * slots, LANES), F32),
    ]


def cost(flops, nbytes):
    return pl.CostEstimate(flops=flops, transcendentals=0, bytes_accessed=nbytes)


def inner(columns, blocks, basis):
    slots, nodes = columns.shape
    parts, modes, _ = basis.shape
    return pl.pallas_call(
        inner_kernel,
        out_shape=pltpu.VMEM((parts, modes, nodes // 2), BF16),
        in_specs=[VMEM_SPEC] * 3,
        out_specs=VMEM_SPEC,
        scratch_shapes=slot_scratch(slots, parts),
        cost_estimate=cost(4 * 10**9, 2 * 10**6),
        compiler_params=PARAMS,
        name="inner",
    )(columns, blocks, in_vmem(basis))


def edge(kernel, columns, blocks, reached, basis, others, image_nodes):
    slots, _ = columns.shape
    parts, modes, halo = reached.shape
    return pl.pallas_call(
        kernel,
        out_shape=pltpu.VMEM((parts, modes, image_nodes), BF16),
        in_specs=[VMEM_SPEC] * (4 + len(others)),
        out_specs=VMEM_SPEC,
        scratch_shapes=slot_scratch(slots, parts) + [pltpu.VMEM((parts * modes, 3 * halo), BF16)],
        cost_estimate=cost(2 * 10**9, 10**6),
        compiler_params=PARAMS,
    )(columns, blocks, in_vmem(reached), in_vmem(basis), *(in_vmem(x) for x in others))


def sampled_kernel(place_ref, inverse_ref, image_ref, out_ref):
    parts, modes, nodes = image_ref.shape
    samples = place_ref.shape[1]
    row_ids = lax.broadcasted_iota(jnp.int32, (16, samples), 0)
    one = jnp.ones((16, samples), BF16)
    zero = jnp.zeros((16, samples), BF16)
    ids = [(row_ids + 16 * q).astype(F32).astype(BF16) for q in range(LANES // 16)]
    place = jnp.broadcast_to(place_ref[...], (16, samples))
    total = jnp.zeros((modes, samples), F32)
    for c in range(parts):
        hits = []
        for first in range(0, nodes, LANES):
            wanted = jnp.clip(place - (c * nodes + first), -1, LANES).astype(F32).astype(BF16)
            hits += [jnp.where(i == wanted, one, zero) for i in ids]
        total = total + jnp.dot(image_ref[c], jnp.concatenate(hits, axis=0), preferred_element_type=F32)
    out_ref[...] = lax.dot_general(
        inverse_ref[...], total.astype(BF16), (((1,), (1,)), ((), ())), preferred_element_type=F32
    )


def sampled(place, inverse, image):
    return pl.pallas_call(
        sampled_kernel,
        in_specs=[VMEM_SPEC] * 3,
        out_shape=pltpu.VMEM((inverse.shape[0], image.shape[1]), F32),
        out_specs=VMEM_SPEC,
        cost_estimate=cost(2 * 10**9, 2 * 10**6),
        compiler_params=PARAMS,
        name="sampled",
    )(place, inverse, in_vmem(image))


def reduced_kernel(basis_ref, mine_ref, theirs_ref, kept_ref, sent_ref):
    chips, parts, modes, nodes = basis_ref.shape
    total = jnp.zeros((chips * modes, 2 * modes), F32)
    for c in range(parts):
        rows = basis_ref[:, c].reshape(chips * modes, nodes)
        both = jnp.concatenate([mine_ref[c], theirs_ref[c]], axis=0)
        total = total + lax.dot_general(rows, both, (((1,), (1,)), ((), ())), preferred_element_type=F32)
    kept_ref[...] = total[:, :modes]
    half = chips * modes // 2
    sent_ref[...] = jnp.concatenate([total[:half, modes:], total[half:, modes:]], axis=1)


def reduced_rows(basis, mine, theirs):
    chips, _, modes, _ = basis.shape
    kept = pltpu.VMEM((chips * modes, modes), F32)
    sent = pltpu.VMEM((chips * modes // 2, 2 * modes), F32)
    return pl.pallas_call(
        reduced_kernel,
        in_specs=[VMEM_SPEC] * 3,
        out_shape=(kept, sent),
        out_specs=(VMEM_SPEC, VMEM_SPEC),
        cost_estimate=cost(2 * 10**9, 2 * 10**6),
        compiler_params=PARAMS,
        name="reduced",
    )(in_vmem(basis), in_vmem(mine), in_vmem(theirs))


def joined_kernel(core_ref, kept_ref, received_ref, sampled_ref, out_ref):
    modes = kept_ref.shape[1]
    core = core_ref[0]
    chips = kept_ref.shape[0] // modes
    for x in range(chips):
        rows = slice(x * modes, (x + 1) * modes)
        side, row = divmod(x, chips // 2)
        packed = (slice(row * modes, (row + 1) * modes), slice(side * modes, (side + 1) * modes))
        for source, left in ((core, kept_ref[rows, :]), (1 - core, received_ref[(1 - core, *packed)])):
            first = pl.multiple_of((2 * x + source) * modes, modes)
            right = sampled_ref[pl.ds(first, modes), :]
            out_ref[pl.ds(first, modes), :] = jnp.concatenate([left, right], axis=1).astype(out_ref.dtype)


def joined(core, kept, received, sampled_part):
    rows, modes = sampled_part.shape
    return pl.pallas_call(
        joined_kernel,
        in_specs=[pl.BlockSpec(memory_space=pltpu.SMEM)] + [VMEM_SPEC] * 3,
        out_shape=pltpu.VMEM((rows, 2 * modes), TRAVEL),
        out_specs=VMEM_SPEC,
        compiler_params=PARAMS,
        name="joined",
    )(core, in_vmem(kept), in_vmem(received), in_vmem(sampled_part))


def total_kernel(scaling, pieces_ref, reduced_ref, coefficients_ref):
    modes = reduced_ref.shape[1]
    total = jnp.sum(pieces_ref[...].astype(F32), axis=0)
    reduced_ref[...] = total[:, :modes] * scaling
    coefficients_ref[...] = total[:, modes:]


def totals(pieces, scaling):
    _, rows, columns = pieces.shape
    out = jax.ShapeDtypeStruct((rows, columns // 2), F32)
    return pl.pallas_call(
        functools.partial(total_kernel, scaling),
        in_specs=[VMEM_SPEC],
        out_shape=(out, out),
        out_specs=(VMEM_SPEC, VMEM_SPEC),
        compiler_params=PARAMS,
        name="totals",
    )(in_vmem(pieces))


def shards(mode_basis, blocks, columns, samples, inverse):
    parts, modes, node_count = mode_basis.shape
    chips = lax.axis_size("x")
    doms = lax.axis_size(DOM)
    dom = lax.axis_index(DOM)
    copies, first, last = spread(mode_basis, chips)
    mine = lax.all_to_all(copies, "x", 0, 0)
    before = lax.ppermute(last, DOM, [(i, (i + 1) % doms) for i in range(doms)])
    after = lax.ppermute(first, DOM, [((i + 1) % doms, i) for i in range(doms)])
    blocks = jnp.transpose(blocks, (1, 2, 0, 3))
    inner_image = inner(columns, blocks, mode_basis)
    left_image = edge(left_kernel, columns, blocks, before, mode_basis, (), node_count // 4)
    others = (left_image, inner_image)
    image = edge(right_kernel, columns, blocks, after, mode_basis, others, node_count)
    node = samples // 3 - dom * node_count
    owned = (node >= 0) & (node < node_count)
    place = jnp.where(owned, (samples % 3) * node_count + node, -1)[None]
    pair = [(0, 1), (1, 0)]
    other_image = lax.ppermute(image, "core", pair)
    sampled_part = sampled(place, inverse, image)
    core = lax.axis_index("core").astype(jnp.int32)[None]
    kept, sent = reduced_rows(mine, image, other_image)
    received = lax.all_gather(sent, "core")
    partial = joined(core, kept, received, sampled_part)
    pieces = lax.all_to_all(partial.reshape(doms, -1, 2 * modes), DOM, 0, 0)
    return totals(pieces, 1.0 / math.sqrt(parts * node_count * doms))


def solution(mesh):
    step_mesh = Mesh(mesh.devices.reshape(4, 16, 4, 2), DOM + MODE)

    return jax.shard_map(
        shards,
        mesh=step_mesh,
        in_specs=(P(None, MODE, DOM), P(None, None, None, DOM), P(None, DOM), P(), P()),
        out_specs=(P(DOM, MODE), P(DOM, MODE)),
        check_vma=False,
    )
```
